32 devices in a mesh: req: 4 (over z), head: 4 (over y, x), blk: 2 (over core).
Axes of the slice: x: 2, y: 2, z: 4, core: 2. Of those that a mesh axis runs over, the one named last changes fastest.
Arguments:
- group_rows: bfloat16 [8, 256, 2048], P(None, 'req', ('head', 'blk')), may hold values from -6 to 6
- slot_request: int32 [8], replicated, may hold values from 0 to 7, each once
- cache_len: int32 [8], replicated, may hold values from 1 to 512, as said below
- group_len: int32 [8], replicated, may hold values from 1 to 256, as said below
- attn_cache: bfloat16 [2, 8, 512, 2048], P(None, 'req', None, ('head', 'blk')), as said below
- hand_cache: bfloat16 [2, 2, 8, 512, 2048], P('blk', None, None, 'req', 'head'), may hold values from -6 to 6
- query_weight: bfloat16 [2048, 2048], P(None, ('head', 'blk')), may hold values from -0.125 to 0.125
- key_weight: bfloat16 [2048, 2048], P(None, ('head', 'blk')), may hold values from -0.125 to 0.125
- value_weight: bfloat16 [2048, 2048], P(None, ('head', 'blk')), may hold values from -0.125 to 0.125
- out_weight: bfloat16 [2048, 2048], P(('head', 'blk')), may hold values from -0.125 to 0.125
- query_gain: float32 [2048], P(('head', 'blk')), may hold values from 0.5 to 1.5
- key_gain: float32 [2048], P(('head', 'blk')), may hold values from 0.5 to 1.5
- attn_gain: float32 [2048], replicated, may hold values from 0.1 to 1.9
- mlp_gain: float32 [2048], replicated, may hold values from 0.1 to 1.9
- gate_weight: bfloat16 [2048, 4096], P(None, ('head', 'blk')), may hold values from -0.125 to 0.125
- up_weight: bfloat16 [2048, 4096], P(None, ('head', 'blk')), may hold values from -0.125 to 0.125
- down_weight: bfloat16 [4096, 2048], P(('head', 'blk')), may hold values from -0.09375 to 0.09375
Outputs:
- layer_out: bfloat16 [8, 256, 2048], P(None, 'req', ('head', 'blk'))
- relaid: bfloat16 [2, 2, 8, 512, 2048], P('blk', None, 'req', None, 'head')
The draws below stay inside these ranges and needn't reach their ends.
Inputs may be any that keep to these rules, and one draw needn't show every extreme that they name: `cache_len`: some request has exactly 512 cached tokens. `group_len`: some request has exactly 256 valid new tokens. `attn_cache`: entry s along the request dimension belongs to request slot_request[s]; positions from cache_len of that request on are not read.
All inputs are finite; a program needn't handle non-finite values.
Results may differ from the reference program's by a relative error of at most 0.009.
The reference program's roundings to bfloat16 on the way (of `ordered`, `keys_new`, `weights`, `attended`, `state`, `inner` and `result`) count: a program that leaves them out, or rounds other values in their place, can miss the bound.
Values may be sent and summed in bfloat16 or wider, within the bound.
A program may use at most 128 MiB of HBM per device.

```python
import jax
import jax.numpy as jnp
from jax import lax

D = 2048
HD = 128
FF = 4096
CTX = 512
GROUP = 256
HAND_LAYERS = 2
REQUESTS = 8


def draw_cache_len(key, part):
    values = jax.random.randint(jax.random.fold_in(key, 11), (REQUESTS,), 1, CTX + 1).astype(jnp.int32)
    where_top = jax.random.randint(jax.random.fold_in(key, 12), (), 0, REQUESTS)
    return values.at[where_top].set(CTX)


def draw_group_len(key, part):
    values = jax.random.randint(jax.random.fold_in(key, 21), (REQUESTS,), 1, GROUP + 1).astype(jnp.int32)
    where_top = jax.random.randint(jax.random.fold_in(key, 22), (), 0, REQUESTS)
    return values.at[where_top].set(GROUP)


def draw_attn_cache(key, part):
    shape = (REQUESTS, CTX, D)
    keys = jax.random.normal(jax.random.fold_in(key, 37), shape, jnp.float32)
    values = jax.random.normal(jax.random.fold_in(key, 38), shape, jnp.float32)
    return jnp.stack([keys, values], axis=0).astype(jnp.bfloat16)


def steps_of(rng, extent, shards, smallest, top_value):
    def one(dim, blocks):
        heights = jax.random.uniform(jax.random.fold_in(jax.random.fold_in(rng, 6), dim), (blocks,), jnp.float32, smallest / len(shards), top_value / len(shards))
        return jnp.repeat(jnp.exp(heights), extent[dim] // blocks).reshape((-1,) + (1,) * (len(extent) - dim - 1))

    loudness = one(*shards[0])
    for cut in shards[1:]:
        loudness = loudness * one(*cut)
    return loudness


def scatter_about(stream_key, dims, deviation, limit, pieces=(), kind=jnp.bfloat16):
    loudness = steps_of(stream_key, dims, pieces, -0.22, 0.18) if pieces else 1.0
    array = jax.random.normal(stream_key, dims, jnp.float32) * deviation * loudness
    return jnp.minimum(jnp.maximum(array, -limit), limit).astype(kind)


def setup_inputs(seed: int = 0) -> dict:
    key_list = jax.random.split(jax.random.key(seed), 18)
    group_rows = scatter_about(key_list[0], (REQUESTS, GROUP, D), 1.0, 6.0, ((1, 4), (2, 8)))
    slot_request = jax.random.permutation(key_list[1], REQUESTS).astype(jnp.int32)
    cache_len = draw_cache_len(jax.random.fold_in(key_list[17], 71), 0)
    group_len = draw_group_len(jax.random.fold_in(key_list[17], 71), 0)
    attn_cache = draw_attn_cache(jax.random.fold_in(key_list[17], 71), 0)
    hand_cache = scatter_about(key_list[5], (HAND_LAYERS, 2, REQUESTS, CTX, D), 1.0, 6.0, ((0, 2), (3, 4), (4, 4)))
    query_weight = scatter_about(key_list[6], (D, D), D ** -0.5, 0.125, ((1, 8),))
    key_weight = scatter_about(key_list[7], (D, D), D ** -0.5, 0.125, ((1, 8),))
    value_weight = scatter_about(key_list[8], (D, D), D ** -0.5, 0.125, ((1, 8),))
    out_weight = scatter_about(key_list[9], (D, D), D ** -0.5, 0.125, ((0, 8),))
    query_gain = jnp.clip(1.0 + 0.1 * jax.random.normal(key_list[10], (D,), jnp.float32), 0.5, 1.5)
    key_gain = jnp.clip(1.0 + 0.1 * jax.random.normal(key_list[11], (D,), jnp.float32), 0.5, 1.5)
    attn_gain = jnp.clip(1.0 + 0.18 * jax.random.normal(key_list[12], (D,), jnp.float32), 0.1, 1.9)
    mlp_gain = jnp.clip(1.0 + 0.18 * jax.random.normal(key_list[13], (D,), jnp.float32), 0.1, 1.9)
    gate_weight = scatter_about(key_list[14], (D, FF), D ** -0.5, 0.125, ((1, 8),))
    up_weight = scatter_about(key_list[15], (D, FF), D ** -0.5, 0.125, ((1, 8),))
    down_weight = scatter_about(key_list[16], (FF, D), FF ** -0.5, 0.09375, ((0, 8),))
    return {"group_rows": group_rows, "slot_request": slot_request, "cache_len": cache_len, "group_len": group_len, "attn_cache": attn_cache, "hand_cache": hand_cache, "query_weight": query_weight, "key_weight": key_weight, "value_weight": value_weight, "out_weight": out_weight, "query_gain": query_gain, "key_gain": key_gain, "attn_gain": attn_gain, "mlp_gain": mlp_gain, "gate_weight": gate_weight, "up_weight": up_weight, "down_weight": down_weight}


EPSILON = 1e-06
ROPE_BASE = 500000.0

def rms_scale(values, gain):
    return values * lax.rsqrt(lax.optimization_barrier(jnp.mean(values * values, axis=-1, keepdims=True)) + EPSILON) * gain

def rotate(values, places):
    half_dim = values.shape[-1] // 2
    frequency = ROPE_BASE ** (-(jnp.arange(half_dim, dtype=jnp.float32) * 2.0 / values.shape[-1]))
    angles = places[..., None].astype(jnp.float32) * frequency
    cosine_part = jnp.cos(angles)[..., None, :]
    sine_part = jnp.sin(angles)[..., None, :]
    first_half = values[..., :half_dim]
    second_half = values[..., half_dim:]
    return jnp.concatenate([first_half * cosine_part - second_half * sine_part, second_half * cosine_part + first_half * sine_part], axis=-1)

def attend(queries, keys_new, values_new, keys_old, values_old, cached, group_valid):
    score_scale = 1.0 / queries.shape[-1] ** 0.5
    span_old = keys_old.shape[1]
    tokens = queries.shape[1]
    old_scores = jnp.einsum('sthd,sjhd->shtj', queries.astype(jnp.float32), keys_old.astype(jnp.float32)) * score_scale
    new_scores = jnp.einsum('sthd,sjhd->shtj', queries.astype(jnp.float32), keys_new.astype(jnp.float32)) * score_scale
    old_mask = (jnp.arange(span_old)[None, :] < cached[:, None])[:, None, None, :]
    columns = jnp.arange(tokens)
    new_mask = (columns[None, None, :] <= columns[None, :, None]) & (columns[None, None, :] < group_valid[:, None, None])
    new_mask = new_mask[:, None, :, :]
    scores = jnp.concatenate([jnp.where(old_mask, old_scores, -1e+30), jnp.where(new_mask, new_scores, -1e+30)], axis=-1)
    row_top = lax.optimization_barrier(jnp.max(scores, axis=-1, keepdims=True))
    weights = jnp.exp(scores - row_top)
    weights = (weights / lax.optimization_barrier(jnp.sum(weights, axis=-1, keepdims=True))).astype(jnp.bfloat16)
    stacked = jnp.concatenate([values_old, values_new], axis=1)
    return jnp.einsum('shtj,sjhd->sthd', weights.astype(jnp.float32), stacked.astype(jnp.float32))

def reference(group_rows, slot_request, cache_len, group_len, attn_cache, hand_cache, query_weight, key_weight, value_weight, out_weight, query_gain, key_gain, attn_gain, mlp_gain, gate_weight, up_weight, down_weight):
    ordered = jnp.take(group_rows, slot_request, axis=0)
    cached = jnp.take(cache_len, slot_request)
    group_valid = jnp.take(group_len, slot_request)
    tokens = ordered.shape[1]
    model_width = ordered.shape[2]
    heads = model_width // HD

    def one_slot(slot_item):
        slot_rows, keys_old, values_old, count_old, count_new = slot_item
        queries = jnp.dot(slot_rows, query_weight, preferred_element_type=jnp.float32)
        keys_new = jnp.dot(slot_rows, key_weight, preferred_element_type=jnp.float32)
        values_new = jnp.dot(slot_rows, value_weight, preferred_element_type=jnp.float32)
        queries = rms_scale(queries, query_gain)
        keys_new = rms_scale(keys_new, key_gain)
        places = count_old + jnp.arange(tokens, dtype=jnp.int32)
        queries = rotate(queries.reshape(tokens, heads, HD), places).astype(jnp.bfloat16)
        keys_new = rotate(keys_new.reshape(tokens, heads, HD), places).astype(jnp.bfloat16)
        values_new = values_new.astype(jnp.bfloat16).reshape(tokens, heads, HD)
        attended = attend(queries[None], keys_new[None], values_new[None], keys_old.reshape(1, -1, heads, HD), values_old.reshape(1, -1, heads, HD), count_old[None], count_new[None])
        return attended.astype(jnp.bfloat16).reshape(tokens, model_width)
    attended = lax.map(one_slot, (ordered, attn_cache[0], attn_cache[1], cached, group_valid))
    projected = jnp.dot(attended.reshape(-1, model_width), out_weight, preferred_element_type=jnp.float32)
    state = (ordered.reshape(-1, model_width).astype(jnp.float32) + rms_scale(projected, attn_gain)).astype(jnp.bfloat16)
    gate_act = jnp.dot(state, gate_weight, preferred_element_type=jnp.float32)
    up_act = jnp.dot(state, up_weight, preferred_element_type=jnp.float32)
    inner = (jax.nn.silu(gate_act) * up_act).astype(jnp.bfloat16)
    down_sum = jnp.dot(inner, down_weight, preferred_element_type=jnp.float32)
    result = (state.astype(jnp.float32) + rms_scale(down_sum, mlp_gain)).astype(jnp.bfloat16).reshape(ordered.shape)
    layer_out = jnp.zeros_like(group_rows).at[slot_request].set(result)
    relaid = jnp.take(hand_cache, slot_request, axis=2)
    return (layer_out, relaid)
```

```python
import functools

import jax
import jax.numpy as jnp
from jax import lax
from jax.experimental import pallas as pl
from jax.experimental.pallas import tpu as pltpu
from jax.sharding import PartitionSpec as P

HD = 128


EPSILON = 1e-06
ROPE_BASE = 500000.0


BF = jnp.bfloat16
F32 = jnp.float32


def layer_kernel(
    dims,
    cached_ref, valid_ref, xt, ht, cos_ref, sin_ref, ac_hbm, wq, wk, wv, wo_hbm, wg, wu, wd_hbm,
    qg, kg, ag, mg,
    out, rel,
    xfull, wqkv, wo, wgu, wd, ac, qkv, stat_mine, stat_all, scale, qb, kb, vb, attended,
    acc, sb1, rb1, sc1, rc1, sb2, rb2, sc2, rc2, stfull, res,
    bsend, xz_recv, h_send, h_recv, lsem, xa_send, xa_recv, st_send, st_recv,
    r1_send, r1_recv, r2_send, r2_recv, sa_send, sa_recv, d1_send, d1_recv, d2_send, d2_recv,
    f_send, f_recv,
):
    nreq, nhead, slots, sc, tokens, tb, w, rows = dims
    model = w * nhead * 2
    rtot = sc * tokens
    r = lax.axis_index("req")
    h = lax.axis_index("head")
    b = lax.axis_index("blk")
    k = h * 2 + b
    other = 1 - b
    span = ht.shape[2]

    def dev(rr, hh, bb):
        return {"req": rr, "head": hh, "blk": bb}

    def rcopy(src, dst, ssem, rsem, rr, hh, bb):
        return pltpu.make_async_remote_copy(
            src_ref=src, dst_ref=dst, send_sem=ssem, recv_sem=rsem,
            device_id=dev(rr, hh, bb), device_id_type=pl.DeviceIdType.MESH,
        )

    barrier = pltpu.get_barrier_semaphore()

    def greet(rr, hh, bb):
        pl.semaphore_signal(
            barrier, inc=1, device_id=dev(rr, hh, bb), device_id_type=pl.DeviceIdType.MESH
        )

    def greet_z(i, carry):
        greet(lax.rem(r + i, nreq), h, b)
        return carry

    lax.fori_loop(1, nreq, greet_z, 0)
    for i in range(1, nhead * 2):
        kk = lax.rem(k + i, nhead * 2)
        greet(r, kk // 2, lax.rem(kk, 2))

    def greet_final(i, carry):
        m = i // nreq
        kk = m * (tokens // rows) + (r * tb) // rows
        rr = lax.rem(i, nreq)

        greet(rr, kk // 2, lax.rem(kk, 2))
        return carry

    lax.fori_loop(0, slots, greet_final, 0)
    first_row = k * rows
    my_slot = first_row // tokens
    my_off = lax.rem(first_row, tokens)
    base_req = my_off // tb
    n_dest = rows // tb
    own_dest = jnp.logical_and(base_req <= r, r < base_req + n_dest)
    locals_ = []

    def load(src, dst, i):
        c = pltpu.make_async_copy(src, dst, lsem.at[i])
        c.start()
        locals_.append(c)

    load(wq, wqkv.at[:, 0:w], 0)
    load(wk, wqkv.at[:, w : 2 * w], 1)
    load(wv, wqkv.at[:, 2 * w : 3 * w], 2)
    load(ac_hbm, ac, 3)
    load(wo_hbm, wo, 4)
    load(wg, wgu.at[:, 0 : wg.shape[1]], 5)
    load(wu, wgu.at[:, wg.shape[1] : 2 * wg.shape[1]], 6)
    load(wd_hbm, wd, 7)
    total = (nreq - 1) + (2 * nhead - 1) + slots
    pl.semaphore_wait(barrier, total)

    my_tok = pl.multiple_of(r * tb, tb)

    def send_x(i, carry):
        rr = lax.rem(r + i, nreq)
        rcopy(
            xt.at[pl.ds(rr * sc, sc)], xfull.at[k, :, pl.ds(my_tok, tb)],
            bsend, xz_recv, rr, h, b,
        ).start()
        return carry

    lax.fori_loop(1, nreq, send_x, 0)
    pltpu.make_async_copy(
        xt.at[pl.ds(r * sc, sc)], xfull.at[k, :, pl.ds(my_tok, tb)], xz_recv
    ).start()
    pltpu.make_async_copy(xfull.at[k], xfull.at[k], xz_recv).wait()

    def gather_send(full, ssem, rsem):
        for d in range(1, nhead):
            rcopy(full.at[k], full.at[k], ssem, rsem.at[k], r, lax.rem(h + d, nhead), b).start()
        rcopy(full.at[k], full.at[k], ssem, rsem.at[k], r, h, other).start()

    def got(full, rsem, kk):
        pltpu.make_async_copy(full.at[kk], full.at[kk], rsem.at[kk]).wait()

    def forward(full, ssem, rsem, d):
        kk = lax.rem(h + nhead - d, nhead) * 2 + b
        got(full, rsem, kk)
        rcopy(full.at[kk], full.at[kk], ssem, rsem.at[kk], r, h, other).start()

    gather_send(xfull, xa_send, xa_recv)

    my_pos = pl.multiple_of(r * span, span)

    def send_h(i, carry):
        rr = lax.rem(r + i, nreq)
        rcopy(
            ht.at[:, pl.ds(rr * sc, sc)], rel.at[:, :, pl.ds(my_pos, span)],
            h_send, h_recv, rr, h, b,
        ).start()
        return carry

    lax.fori_loop(1, nreq, send_h, 0)
    pltpu.make_async_copy(
        ht.at[:, pl.ds(r * sc, sc)], rel.at[:, :, pl.ds(my_pos, span)], h_recv
    ).start()

    for d in range(1, nhead):
        forward(xfull, xa_send, xa_recv, d)
    for d in range(nhead):
        got(xfull, xa_recv, lax.rem(h + nhead - d, nhead) * 2 + other)
    for c in locals_[:3]:
        c.wait()

    tile = 128
    per_slot = tokens // tile

    def project(i, carry):
        s = i // per_slot
        at = pl.multiple_of(lax.rem(i, per_slot) * tile, tile)
        here = pl.multiple_of(i * tile, tile)
        x = jnp.concatenate(
            [xfull[kk, s, pl.ds(at, tile), :] for kk in range(2 * nhead)], axis=1
        )
        y = jnp.dot(x, wqkv[...], preferred_element_type=F32)
        qkv[pl.ds(here, tile), :] = y
        q, kn = y[:, :w], y[:, w : 2 * w]
        lanes = lax.broadcasted_iota(jnp.int32, (tile, tile), 1)
        sums = jnp.where(
            lanes == 0,
            jnp.sum(q * q, axis=1, keepdims=True),
            jnp.where(lanes == 1, jnp.sum(kn * kn, axis=1, keepdims=True), 0.0),
        )
        stat_mine[i] = sums.T[0:8, :]
        return carry

    lax.fori_loop(0, rtot // tile, project, 0)
    for i in range(1, 2 * nhead):
        kk = lax.rem(k + i, 2 * nhead)
        rcopy(
            stat_mine, stat_all.at[k], st_send, st_recv.at[k], r, kk // 2, lax.rem(kk, 2)
        ).start()
    stat_all[k] = stat_mine[...]
    for i in range(1, 2 * nhead):
        kk = lax.rem(k + i, 2 * nhead)
        pltpu.make_async_copy(stat_all.at[kk], stat_all.at[kk], st_recv.at[kk]).wait()
    scale[...] = lax.rsqrt(jnp.sum(stat_all[...], axis=0) / model + EPSILON)

    heads_here = w // HD

    def finish(i, carry):
        here = pl.multiple_of(i * tile, tile)
        sq = jnp.concatenate([scale[i], jnp.zeros((tile - 8, tile), F32)], axis=0).T
        cosv = cos_ref[pl.ds(here, tile), :]
        sinv = sin_ref[pl.ds(here, tile), :]
        q = qkv[pl.ds(here, tile), 0:w] * sq[:, 0:1] * qg[...]
        kn = qkv[pl.ds(here, tile), w : 2 * w] * sq[:, 1:2] * kg[...]
        for hh in range(heads_here):
            cut = slice(hh * HD, (hh + 1) * HD)
            qh, kh = q[:, cut], kn[:, cut]
            qb[pl.ds(here, tile), cut] = (qh * cosv + pltpu.roll(qh, HD // 2, 1) * sinv).astype(BF)
            kb[pl.ds(here, tile), cut] = (kh * cosv + pltpu.roll(kh, HD // 2, 1) * sinv).astype(BF)
        vb[pl.ds(here, tile), :] = qkv[pl.ds(here, tile), 2 * w : 3 * w].astype(BF)
        return carry

    lax.fori_loop(0, rtot // tile, finish, 0)
    locals_[3].wait()
    score_scale = 1.0 / HD**0.5
    ctx = ac.shape[2]
    nt = (((1,), (1,)), ((), ()))

    def attend(i, carry):
        s = i // per_slot
        at = lax.rem(i, per_slot) * tile
        here = pl.multiple_of(i * tile, tile)
        there = pl.multiple_of(s * tokens, tokens)
        old_ok = lax.broadcasted_iota(jnp.int32, (tile, ctx), 1) < cached_ref[s]
        col = lax.broadcasted_iota(jnp.int32, (tile, tokens), 1)
        row = lax.broadcasted_iota(jnp.int32, (tile, tokens), 0) + at
        new_ok = jnp.logical_and(col <= row, col < valid_ref[s])
        for hh in range(heads_here):
            cut = slice(hh * HD, (hh + 1) * HD)
            q = qb[pl.ds(here, tile), cut]
            so = lax.dot_general(q, ac[0, s, :, cut], nt, preferred_element_type=F32) * score_scale
            sn = (
                lax.dot_general(q, kb[pl.ds(there, tokens), cut], nt, preferred_element_type=F32)
                * score_scale
            )
            so = jnp.where(old_ok, so, -1e30)
            sn = jnp.where(new_ok, sn, -1e30)
            top = jnp.maximum(
                jnp.max(so, axis=1, keepdims=True), jnp.max(sn, axis=1, keepdims=True)
            )
            po, pn = jnp.exp(so - top), jnp.exp(sn - top)
            inv = 1.0 / (jnp.sum(po, axis=1, keepdims=True) + jnp.sum(pn, axis=1, keepdims=True))
            o = jnp.dot(
                (po * inv).astype(BF), ac[1, s, :, cut], preferred_element_type=F32
            ) + jnp.dot(
                (pn * inv).astype(BF), vb[pl.ds(there, tokens), cut], preferred_element_type=F32
            )
            attended[pl.ds(here, tile), cut] = o.astype(BF)
        return carry

    lax.fori_loop(0, rtot // tile, attend, 0)
    locals_[4].wait()

    def pair_send(hh, p0, p1, sb, rb, ssem, rsem):
        mine = jnp.where(b == 0, p0, p1)
        theirs = jnp.where(b == 0, p1, p0)
        acc[hh] = mine
        sb[hh] = theirs.astype(BF)
        rcopy(sb.at[hh], rb.at[hh], ssem, rsem.at[hh], r, h, other).start()

    def chip_send(hh, d, rb, sc_, rc_, rsem, ssem2, rsem2):
        pltpu.make_async_copy(rb.at[hh], rb.at[hh], rsem.at[hh]).wait()
        total = acc[hh] + rb[hh].astype(F32)
        if d == 0:
            acc[hh] = total
        else:
            sc_[hh] = total.astype(BF)
            rcopy(sc_.at[hh], rc_.at[h], ssem2, rsem2.at[h], r, hh, b).start()

    def collect(rc_, rsem2):
        value = acc[h]
        for d in range(1, nhead):
            hh = lax.rem(h + nhead - d, nhead)
            pltpu.make_async_copy(rc_.at[hh], rc_.at[hh], rsem2.at[hh]).wait()
            value = value + rc_[hh].astype(F32)
        return value

    order = list(range(1, nhead)) + [0]
    for d in order:
        hh = lax.rem(h + d, nhead)
        at = pl.multiple_of(hh * 2 * rows, 2 * rows)
        p = jnp.dot(attended[pl.ds(at, 2 * rows), :], wo[...], preferred_element_type=F32)
        pair_send(hh, p[:rows], p[rows:], sb1, rb1, r1_send, r1_recv)
    for d in order:
        chip_send(lax.rem(h + d, nhead), d, rb1, sc1, rc1, r1_recv, r2_send, r2_recv)
    proj = collect(rc1, r2_recv)
    x_rows = jnp.concatenate(
        [xfull[kk, my_slot, pl.ds(pl.multiple_of(my_off, rows), rows), :] for kk in range(2 * nhead)],
        axis=1,
    ).astype(F32)
    norm = lax.rsqrt(jnp.mean(proj * proj, axis=1, keepdims=True) + EPSILON)
    stfull[k] = (x_rows + proj * norm * ag[...]).astype(BF)
    gather_send(stfull, sa_send, sa_recv)
    for c in locals_[5:]:
        c.wait()
    ff = wd.shape[0]

    def mlp(hh):
        s = jnp.concatenate([stfull[2 * hh], stfull[2 * hh + 1]], axis=0)
        gu = jnp.dot(s, wgu[...], preferred_element_type=F32)
        g, u = gu[:, :ff], gu[:, ff:]
        inner = (g * jax.nn.sigmoid(g) * u).astype(BF)
        p = jnp.dot(inner, wd[...], preferred_element_type=F32)
        pair_send(hh, p[:rows], p[rows:], sb2, rb2, d1_send, d1_recv)

    got(stfull, sa_recv, h * 2 + other)
    mlp(h)
    for d in range(1, nhead):
        forward(stfull, sa_send, sa_recv, d)
    for d in range(1, nhead):
        hh = lax.rem(h + nhead - d, nhead)
        got(stfull, sa_recv, hh * 2 + other)
        mlp(hh)
        chip_send(hh, d, rb2, sc2, rc2, d1_recv, d2_send, d2_recv)
    chip_send(h, 0, rb2, sc2, rc2, d1_recv, d2_send, d2_recv)
    down = collect(rc2, d2_recv)
    norm = lax.rsqrt(jnp.mean(down * down, axis=1, keepdims=True) + EPSILON)
    result = (stfull[k].astype(F32) + down * norm * mg[...]).astype(BF)
    for kk in range(2 * nhead):
        for i in range(n_dest):
            res[i, kk] = result[i * tb : (i + 1) * tb, kk * w : (kk + 1) * w]
    slot = r * sc + my_slot

    def send_home(i, carry):
        kk = lax.rem(k + i // n_dest, 2 * nhead)
        part = lax.rem(i, n_dest)
        rr = base_req + part
        mine = jnp.logical_and(rr == r, kk == k)

        @pl.when(mine)
        def _():
            c = pltpu.make_async_copy(res.at[part, kk], out.at[slot], f_recv)
            c.start()

        @pl.when(jnp.logical_not(mine))
        def _():
            rcopy(
                res.at[part, kk], out.at[slot], f_send, f_recv, rr, kk // 2, lax.rem(kk, 2)
            ).start()

        return carry

    lax.fori_loop(0, 2 * nhead * n_dest, send_home, 0)

    pltpu.make_async_copy(out, out, f_recv).wait()
    pltpu.make_async_copy(rel, rel, h_recv).wait()

    def drain(ref, sem):
        pltpu.make_async_copy(ref, ref, sem).wait()

    if nreq > 1:
        drain(xt.at[pl.ds(0, (nreq - 1) * sc)], bsend)
        drain(ht.at[:, pl.ds(0, (nreq - 1) * sc)], h_send)
    drain(xfull.at[pl.ds(0, 2 * nhead - 1)], xa_send)
    drain(stfull.at[pl.ds(0, 2 * nhead - 1)], sa_send)
    drain(stat_all.at[pl.ds(0, 2 * nhead - 1)], st_send)
    drain(sb1, r1_send)
    drain(sb2, d1_send)
    drain(sc1.at[pl.ds(0, nhead - 1)], r2_send)
    drain(sc2.at[pl.ds(0, nhead - 1)], d2_send)

    sent = res.shape[0] * res.shape[1]

    @pl.when(own_dest)
    def _():
        drain(out.at[pl.ds(0, sent - 1)], f_send)

    @pl.when(jnp.logical_not(own_dest))
    def _():
        drain(out.at[pl.ds(0, sent)], f_send)


def on_device(
    group_rows,
    slot_request,
    cache_len,
    group_len,
    attn_cache,
    hand_cache,
    query_weight,
    key_weight,
    value_weight,
    out_weight,
    query_gain,
    key_gain,
    attn_gain,
    mlp_gain,
    gate_weight,
    up_weight,
    down_weight,
):
    nreq = lax.axis_size("req")
    nhead = lax.axis_size("head")
    slots, tb, w = group_rows.shape
    sc = slots // nreq
    tokens = tb * nreq
    rows = sc * tokens // (2 * nhead)
    own_requests = lax.dynamic_slice_in_dim(slot_request, lax.axis_index("req") * sc, sc)
    cached = jnp.take(cache_len, own_requests)
    valid = jnp.take(group_len, own_requests)
    inverse = (
        jnp.zeros_like(slot_request).at[slot_request].set(jnp.arange(slots, dtype=jnp.int32))
    )
    xt = jnp.take(group_rows, slot_request, axis=0)
    ht = jnp.take(hand_cache[0], slot_request, axis=1)
    places = (cached[:, None] + jnp.arange(tokens, dtype=jnp.int32)[None, :]).reshape(-1)
    half = HD // 2
    frequency = ROPE_BASE ** (-(jnp.arange(half, dtype=F32) * 2.0 / HD))
    angles = places[:, None].astype(F32) * frequency
    cosv, sinv = jnp.cos(angles), jnp.sin(angles)
    cosv = jnp.concatenate([cosv, cosv], axis=1)
    sinv = jnp.concatenate([-sinv, sinv], axis=1)
    model = w * nhead * 2
    ff = gate_weight.shape[1]
    span = ht.shape[2]
    rtot = sc * tokens
    n8 = 2 * nhead
    dims = (nreq, nhead, slots, sc, tokens, tb, w, rows)
    dma = pltpu.SemaphoreType.DMA
    vm = pl.BlockSpec(memory_space=pltpu.VMEM)
    hb = pl.BlockSpec(memory_space=pl.ANY)
    sm = pl.BlockSpec(memory_space=pltpu.SMEM)
    blocks = lambda n: pltpu.VMEM((n, rows, model), BF)
    out, rel = pl.pallas_call(
        functools.partial(layer_kernel, dims),
        out_shape=(
            jax.ShapeDtypeStruct((slots, tb, w), BF),
            jax.ShapeDtypeStruct((ht.shape[0], sc, span * nreq, ht.shape[3]), BF),
        ),
        in_specs=[sm, sm, vm, hb, vm, vm, hb, hb, hb, hb, hb, hb, hb, hb, vm, vm, vm, vm],
        out_specs=(vm, hb),
        scratch_shapes=[
            pltpu.VMEM((n8, sc, tokens, w), BF),
            pltpu.VMEM((model, 3 * w), BF),
            pltpu.VMEM((w, model), BF),
            pltpu.VMEM((model, 2 * ff), BF),
            pltpu.VMEM((ff, model), BF),
            pltpu.VMEM(attn_cache.shape, BF),
            pltpu.VMEM((rtot, 3 * w), F32),
            pltpu.VMEM((rtot // 128, 8, 128), F32),
            pltpu.VMEM((n8, rtot // 128, 8, 128), F32),
            pltpu.VMEM((rtot // 128, 8, 128), F32),
            pltpu.VMEM((rtot, w), BF),
            pltpu.VMEM((rtot, w), BF),
            pltpu.VMEM((rtot, w), BF),
            pltpu.VMEM((rtot, w), BF),
            pltpu.VMEM((nhead, rows, model), F32),
            blocks(nhead), blocks(nhead), blocks(nhead), blocks(nhead),
            blocks(nhead), blocks(nhead), blocks(nhead), blocks(nhead),
            blocks(n8),
            pltpu.VMEM((rows // tb, n8, tb, w), BF),
            dma, dma, dma, dma, dma((8,)), dma, dma((n8,)), dma, dma((n8,)),
            dma, dma((nhead,)), dma, dma((nhead,)), dma, dma((n8,)),
            dma, dma((nhead,)), dma, dma((nhead,)),
            dma, dma,
        ],
        compiler_params=pltpu.CompilerParams(
            collective_id=0, has_side_effects=True, vmem_limit_bytes=56 * 1024 * 1024
        ),
    )(
        cached, valid, xt, ht, cosv, sinv, attn_cache, query_weight, key_weight, value_weight,
        out_weight, gate_weight, up_weight, down_weight,
        query_gain[None], key_gain[None], attn_gain[None], mlp_gain[None],
    )
    return (jnp.take(out, inverse, axis=0), rel[None])


def solution(mesh):
    in_specs = (
        P(None, "req", ("head", "blk")),
        P(),
        P(),
        P(),
        P(None, "req", None, ("head", "blk")),
        P("blk", None, None, "req", "head"),
        P(None, ("head", "blk")),
        P(None, ("head", "blk")),
        P(None, ("head", "blk")),
        P(("head", "blk"), None),
        P(("head", "blk")),
        P(("head", "blk")),
        P(),
        P(),
        P(None, ("head", "blk")),
        P(None, ("head", "blk")),
        P(("head", "blk"), None),
    )
    out_specs = (P(None, "req", ("head", "blk")), P("blk", None, "req", None, "head"))
    return jax.shard_map(
        on_device, mesh=mesh, in_specs=in_specs, out_specs=out_specs, check_vma=False
    )
```

```python
import functools

import jax
import jax.numpy as jnp
from jax import lax
from jax.experimental import pallas as pl
from jax.experimental.pallas import tpu as pltpu
from jax.sharding import PartitionSpec as P

HD = 128


EPSILON = 1e-06
ROPE_BASE = 500000.0


BF = jnp.bfloat16
F32 = jnp.float32


def layer_kernel(
    dims,
    slot_ref, clen_ref, glen_ref, group, hand, freq, ac_hbm, wq, wk, wv, wo_hbm, wg, wu, wd_hbm,
    qg, kg, ag, mg,
    landed, rel,
    xfull, wqkv, wo, wgu, wd, ac, qkv, stat_mine, stat_all, scale, qb, kb, vb, attended,
    xt, ht_in, ht, cos_ref, sin_ref, acc, sb1, rb1, sc1, rc1, sb2, rb2, sc2, rc2, stfull, res,
    bsend, xz_recv, h_send, h_recv, lsem, xa_send, xa_recv, st_send, st_recv,
    r1_send, r1_recv, r2_send, r2_recv, sa_send, sa_recv, d1_send, d1_recv, d2_send, d2_recv,
    f_send, f_recv,
):
    nreq, nhead, slots, sc, tokens, tb, w, rows = dims
    model = w * nhead * 2
    rtot = sc * tokens
    r = lax.axis_index("req")
    h = lax.axis_index("head")
    b = lax.axis_index("blk")
    k = h * 2 + b
    other = 1 - b
    span = ht.shape[2]

    def dev(rr, hh, bb):
        return {"req": rr, "head": hh, "blk": bb}

    def rcopy(src, dst, ssem, rsem, rr, hh, bb):
        return pltpu.make_async_remote_copy(
            src_ref=src, dst_ref=dst, send_sem=ssem, recv_sem=rsem,
            device_id=dev(rr, hh, bb), device_id_type=pl.DeviceIdType.MESH,
        )

    barrier = pltpu.get_barrier_semaphore()

    def greet(rr, hh, bb):
        pl.semaphore_signal(
            barrier, inc=1, device_id=dev(rr, hh, bb), device_id_type=pl.DeviceIdType.MESH
        )

    def greet_z(i, carry):
        greet(lax.rem(r + i, nreq), h, b)
        return carry

    lax.fori_loop(1, nreq, greet_z, 0)
    for i in range(1, nhead * 2):
        kk = lax.rem(k + i, nhead * 2)
        greet(r, kk // 2, lax.rem(kk, 2))

    def greet_final(i, carry):
        m = i // nreq
        kk = m * (tokens // rows) + (r * tb) // rows
        rr = lax.rem(i, nreq)

        greet(rr, kk // 2, lax.rem(kk, 2))
        return carry

    lax.fori_loop(0, slots, greet_final, 0)
    first_row = k * rows
    my_slot = first_row // tokens
    my_off = lax.rem(first_row, tokens)
    base_req = my_off // tb
    n_dest = rows // tb
    own_dest = jnp.logical_and(base_req <= r, r < base_req + n_dest)
    locals_ = []

    def load(src, dst, i):
        c = pltpu.make_async_copy(src, dst, lsem.at[i])
        c.start()
        locals_.append(c)

    load(wq, wqkv.at[:, 0:w], 0)
    load(wk, wqkv.at[:, w : 2 * w], 1)
    load(wv, wqkv.at[:, 2 * w : 3 * w], 2)
    load(ac_hbm, ac, 3)
    load(wo_hbm, wo, 4)
    load(wg, wgu.at[:, 0 : wg.shape[1]], 5)
    load(wu, wgu.at[:, wg.shape[1] : 2 * wg.shape[1]], 6)
    load(wd_hbm, wd, 7)
    load(hand, ht_in, 8)

    def order_x(i, carry):
        xt[i] = group[slot_ref[i]]
        return carry

    lax.fori_loop(0, slots, order_x, 0)
    total = (nreq - 1) + (2 * nhead - 1) + slots
    pl.semaphore_wait(barrier, total)

    my_tok = pl.multiple_of(r * tb, tb)

    def send_x(i, carry):
        rr = lax.rem(r + i, nreq)
        rcopy(
            xt.at[pl.ds(rr * sc, sc)], xfull.at[k, :, pl.ds(my_tok, tb)],
            bsend, xz_recv, rr, h, b,
        ).start()
        return carry

    lax.fori_loop(1, nreq, send_x, 0)
    pltpu.make_async_copy(
        xt.at[pl.ds(r * sc, sc)], xfull.at[k, :, pl.ds(my_tok, tb)], xz_recv
    ).start()
    pltpu.make_async_copy(xfull.at[k], xfull.at[k], xz_recv).wait()

    def gather_send(full, ssem, rsem):
        for d in range(1, nhead):
            rcopy(full.at[k], full.at[k], ssem, rsem.at[k], r, lax.rem(h + d, nhead), b).start()
        rcopy(full.at[k], full.at[k], ssem, rsem.at[k], r, h, other).start()

    def got(full, rsem, kk):
        pltpu.make_async_copy(full.at[kk], full.at[kk], rsem.at[kk]).wait()

    def forward(full, ssem, rsem, d):
        kk = lax.rem(h + nhead - d, nhead) * 2 + b
        got(full, rsem, kk)
        rcopy(full.at[kk], full.at[kk], ssem, rsem.at[kk], r, h, other).start()

    gather_send(xfull, xa_send, xa_recv)

    my_pos = pl.multiple_of(r * span, span)
    locals_[8].wait()
    step = min(span, 32)

    def order_h(i, carry):
        s = i // (span // step)
        at = pl.multiple_of(lax.rem(i, span // step) * step, step)
        for c in range(hand.shape[0]):
            ht[c, s, pl.ds(at, step), :] = ht_in[c, slot_ref[s], pl.ds(at, step), :]
        return carry

    lax.fori_loop(0, slots * (span // step), order_h, 0)

    def send_h(i, carry):
        rr = lax.rem(r + i, nreq)
        rcopy(
            ht.at[:, pl.ds(rr * sc, sc)], rel.at[:, :, pl.ds(my_pos, span)],
            h_send, h_recv, rr, h, b,
        ).start()
        return carry

    lax.fori_loop(1, nreq, send_h, 0)
    pltpu.make_async_copy(
        ht.at[:, pl.ds(r * sc, sc)], rel.at[:, :, pl.ds(my_pos, span)], h_recv
    ).start()

    half = HD // 2

    def angles(i, carry):
        here = pl.multiple_of(i * 128, 128)
        s = i // (tokens // 128)
        start = clen_ref[slot_ref[r * sc + s]] + lax.rem(i, tokens // 128) * 128
        place = lax.broadcasted_iota(jnp.int32, (128, HD), 0) + start
        lane = lax.broadcasted_iota(jnp.int32, (128, HD), 1)
        angle = place.astype(F32) * freq[...]
        cos_ref[pl.ds(here, 128), :] = jnp.cos(angle)
        sine = jnp.sin(angle)
        sin_ref[pl.ds(here, 128), :] = jnp.where(lane < half, -sine, sine)
        return carry

    lax.fori_loop(0, rtot // 128, angles, 0)

    tile = 128
    per_slot = tokens // tile

    for d in range(1, nhead):
        forward(xfull, xa_send, xa_recv, d)
    for d in range(nhead):
        got(xfull, xa_recv, lax.rem(h + nhead - d, nhead) * 2 + other)
    for c in locals_[:3]:
        c.wait()

    def project(i, carry):
        s = i // per_slot
        at = pl.multiple_of(lax.rem(i, per_slot) * tile, tile)
        here = pl.multiple_of(i * tile, tile)
        x = jnp.concatenate(
            [xfull[kk, s, pl.ds(at, tile), :] for kk in range(2 * nhead)], axis=1
        )
        y = jnp.dot(x, wqkv[...], preferred_element_type=F32)
        qkv[pl.ds(here, tile), :] = y
        q, kn = y[:, :w], y[:, w : 2 * w]
        lanes = lax.broadcasted_iota(jnp.int32, (tile, tile), 1)
        sums = jnp.where(
            lanes == 0,
            jnp.sum(q * q, axis=1, keepdims=True),
            jnp.where(lanes == 1, jnp.sum(kn * kn, axis=1, keepdims=True), 0.0),
        )
        stat_mine[i] = sums.T[0:8, :]
        return carry

    lax.fori_loop(0, rtot // tile, project, 0)
    for i in range(1, 2 * nhead):
        kk = lax.rem(k + i, 2 * nhead)
        rcopy(
            stat_mine, stat_all.at[k], st_send, st_recv.at[k], r, kk // 2, lax.rem(kk, 2)
        ).start()
    stat_all[k] = stat_mine[...]
    for i in range(1, 2 * nhead):
        kk = lax.rem(k + i, 2 * nhead)
        pltpu.make_async_copy(stat_all.at[kk], stat_all.at[kk], st_recv.at[kk]).wait()
    scale[...] = lax.rsqrt(jnp.sum(stat_all[...], axis=0) / model + EPSILON)

    heads_here = w // HD

    def finish(i, carry):
        here = pl.multiple_of(i * tile, tile)
        sq = jnp.concatenate([scale[i], jnp.zeros((tile - 8, tile), F32)], axis=0).T
        cosv = cos_ref[pl.ds(here, tile), :]
        sinv = sin_ref[pl.ds(here, tile), :]
        q = qkv[pl.ds(here, tile), 0:w] * sq[:, 0:1] * qg[...]
        kn = qkv[pl.ds(here, tile), w : 2 * w] * sq[:, 1:2] * kg[...]
        for hh in range(heads_here):
            cut = slice(hh * HD, (hh + 1) * HD)
            qh, kh = q[:, cut], kn[:, cut]
            qb[pl.ds(here, tile), cut] = (qh * cosv + pltpu.roll(qh, HD // 2, 1) * sinv).astype(BF)
            kb[pl.ds(here, tile), cut] = (kh * cosv + pltpu.roll(kh, HD // 2, 1) * sinv).astype(BF)
        vb[pl.ds(here, tile), :] = qkv[pl.ds(here, tile), 2 * w : 3 * w].astype(BF)
        return carry

    lax.fori_loop(0, rtot // tile, finish, 0)
    locals_[3].wait()
    score_scale = 1.0 / HD**0.5
    ctx = ac.shape[2]
    nt = (((1,), (1,)), ((), ()))

    def attend(i, carry):
        s = i // per_slot
        at = lax.rem(i, per_slot) * tile
        here = pl.multiple_of(i * tile, tile)
        there = pl.multiple_of(s * tokens, tokens)
        old_ok = lax.broadcasted_iota(jnp.int32, (tile, ctx), 1) < clen_ref[slot_ref[r * sc + s]]
        col = lax.broadcasted_iota(jnp.int32, (tile, tokens), 1)
        row = lax.broadcasted_iota(jnp.int32, (tile, tokens), 0) + at
        new_ok = jnp.logical_and(col <= row, col < glen_ref[slot_ref[r * sc + s]])
        for hh in range(heads_here):
            cut = slice(hh * HD, (hh + 1) * HD)
            q = qb[pl.ds(here, tile), cut]
            so = lax.dot_general(q, ac[0, s, :, cut], nt, preferred_element_type=F32) * score_scale
            sn = (
                lax.dot_general(q, kb[pl.ds(there, tokens), cut], nt, preferred_element_type=F32)
                * score_scale
            )
            so = jnp.where(old_ok, so, -1e30)
            sn = jnp.where(new_ok, sn, -1e30)
            top = jnp.maximum(
                jnp.max(so, axis=1, keepdims=True), jnp.max(sn, axis=1, keepdims=True)
            )
            po, pn = jnp.exp(so - top), jnp.exp(sn - top)
            inv = 1.0 / (jnp.sum(po, axis=1, keepdims=True) + jnp.sum(pn, axis=1, keepdims=True))
            o = jnp.dot(
                (po * inv).astype(BF), ac[1, s, :, cut], preferred_element_type=F32
            ) + jnp.dot(
                (pn * inv).astype(BF), vb[pl.ds(there, tokens), cut], preferred_element_type=F32
            )
            attended[pl.ds(here, tile), cut] = o.astype(BF)
        return carry

    lax.fori_loop(0, rtot // tile, attend, 0)
    locals_[4].wait()

    def pair_send(hh, p0, p1, sb, rb, ssem, rsem):
        mine = jnp.where(b == 0, p0, p1)
        theirs = jnp.where(b == 0, p1, p0)
        acc[hh] = mine
        sb[hh] = theirs.astype(BF)
        rcopy(sb.at[hh], rb.at[hh], ssem, rsem.at[hh], r, h, other).start()

    def chip_send(hh, d, rb, sc_, rc_, rsem, ssem2, rsem2):
        pltpu.make_async_copy(rb.at[hh], rb.at[hh], rsem.at[hh]).wait()
        total = acc[hh] + rb[hh].astype(F32)
        if d == 0:
            acc[hh] = total
        else:
            sc_[hh] = total.astype(BF)
            rcopy(sc_.at[hh], rc_.at[h], ssem2, rsem2.at[h], r, hh, b).start()

    def collect(rc_, rsem2):
        value = acc[h]
        for d in range(1, nhead):
            hh = lax.rem(h + nhead - d, nhead)
            pltpu.make_async_copy(rc_.at[hh], rc_.at[hh], rsem2.at[hh]).wait()
            value = value + rc_[hh].astype(F32)
        return value

    order = list(range(1, nhead)) + [0]
    for d in order:
        hh = lax.rem(h + d, nhead)
        at = pl.multiple_of(hh * 2 * rows, 2 * rows)
        p = jnp.dot(attended[pl.ds(at, 2 * rows), :], wo[...], preferred_element_type=F32)
        pair_send(hh, p[:rows], p[rows:], sb1, rb1, r1_send, r1_recv)
    for d in order:
        chip_send(lax.rem(h + d, nhead), d, rb1, sc1, rc1, r1_recv, r2_send, r2_recv)
    proj = collect(rc1, r2_recv)
    x_rows = jnp.concatenate(
        [xfull[kk, my_slot, pl.ds(pl.multiple_of(my_off, rows), rows), :] for kk in range(2 * nhead)],
        axis=1,
    ).astype(F32)
    norm = lax.rsqrt(jnp.mean(proj * proj, axis=1, keepdims=True) + EPSILON)
    stfull[k] = (x_rows + proj * norm * ag[...]).astype(BF)
    gather_send(stfull, sa_send, sa_recv)
    for c in locals_[5:8]:
        c.wait()
    ff = wd.shape[0]

    def mlp(hh):
        s = jnp.concatenate([stfull[2 * hh], stfull[2 * hh + 1]], axis=0)
        gu = jnp.dot(s, wgu[...], preferred_element_type=F32)
        g, u = gu[:, :ff], gu[:, ff:]
        inner = (g * jax.nn.sigmoid(g) * u).astype(BF)
        p = jnp.dot(inner, wd[...], preferred_element_type=F32)
        pair_send(hh, p[:rows], p[rows:], sb2, rb2, d1_send, d1_recv)

    got(stfull, sa_recv, h * 2 + other)
    mlp(h)
    for d in range(1, nhead):
        forward(stfull, sa_send, sa_recv, d)
    for d in range(1, nhead):
        hh = lax.rem(h + nhead - d, nhead)
        got(stfull, sa_recv, hh * 2 + other)
        mlp(hh)
        chip_send(hh, d, rb2, sc2, rc2, d1_recv, d2_send, d2_recv)
    chip_send(h, 0, rb2, sc2, rc2, d1_recv, d2_send, d2_recv)
    down = collect(rc2, d2_recv)
    norm = lax.rsqrt(jnp.mean(down * down, axis=1, keepdims=True) + EPSILON)
    result = (stfull[k].astype(F32) + down * norm * mg[...]).astype(BF)
    for kk in range(2 * nhead):
        for i in range(n_dest):
            res[i, kk] = result[i * tb : (i + 1) * tb, kk * w : (kk + 1) * w]
    slot = r * sc + my_slot

    def send_home(i, carry):
        kk = lax.rem(k + i // n_dest, 2 * nhead)
        part = lax.rem(i, n_dest)
        rr = base_req + part
        mine = jnp.logical_and(rr == r, kk == k)

        @pl.when(mine)
        def _():
            c = pltpu.make_async_copy(res.at[part, kk], landed.at[slot], f_recv)
            c.start()

        @pl.when(jnp.logical_not(mine))
        def _():
            rcopy(
                res.at[part, kk], landed.at[slot], f_send, f_recv, rr, kk // 2, lax.rem(kk, 2)
            ).start()

        return carry

    lax.fori_loop(0, 2 * nhead * n_dest, send_home, 0)

    pltpu.make_async_copy(landed, landed, f_recv).wait()
    pltpu.make_async_copy(rel, rel, h_recv).wait()

    def drain(ref, sem):
        pltpu.make_async_copy(ref, ref, sem).wait()

    if nreq > 1:
        drain(xt.at[pl.ds(0, (nreq - 1) * sc)], bsend)
        drain(ht.at[:, pl.ds(0, (nreq - 1) * sc)], h_send)
    drain(xfull.at[pl.ds(0, 2 * nhead - 1)], xa_send)
    drain(stfull.at[pl.ds(0, 2 * nhead - 1)], sa_send)
    drain(stat_all.at[pl.ds(0, 2 * nhead - 1)], st_send)
    drain(sb1, r1_send)
    drain(sb2, d1_send)
    drain(sc1.at[pl.ds(0, nhead - 1)], r2_send)
    drain(sc2.at[pl.ds(0, nhead - 1)], d2_send)

    sent = res.shape[0] * res.shape[1]

    @pl.when(own_dest)
    def _():
        drain(landed.at[pl.ds(0, sent - 1)], f_send)

    @pl.when(jnp.logical_not(own_dest))
    def _():
        drain(landed.at[pl.ds(0, sent)], f_send)


def home_kernel(slot_ref, landed, home):
    def one(s, carry):
        home[slot_ref[s]] = landed[s]
        return carry

    lax.fori_loop(0, landed.shape[0], one, 0)


def on_device(
    group_rows,
    slot_request,
    cache_len,
    group_len,
    attn_cache,
    hand_cache,
    query_weight,
    key_weight,
    value_weight,
    out_weight,
    query_gain,
    key_gain,
    attn_gain,
    mlp_gain,
    gate_weight,
    up_weight,
    down_weight,
):
    nreq = lax.axis_size("req")
    nhead = lax.axis_size("head")
    slots, tb, w = group_rows.shape
    sc = slots // nreq
    tokens = tb * nreq
    rows = sc * tokens // (2 * nhead)
    half = HD // 2
    frequency = ROPE_BASE ** (-(jnp.arange(half, dtype=F32) * 2.0 / HD))
    freq = jnp.concatenate([frequency, frequency])[None]
    hand = hand_cache[0]
    model = w * nhead * 2
    ff = gate_weight.shape[1]
    span = hand.shape[2]
    rtot = sc * tokens
    n8 = 2 * nhead
    dims = (nreq, nhead, slots, sc, tokens, tb, w, rows)
    dma = pltpu.SemaphoreType.DMA
    vm = pl.BlockSpec(memory_space=pltpu.VMEM)
    hb = pl.BlockSpec(memory_space=pl.ANY)
    sm = pl.BlockSpec(memory_space=pltpu.SMEM)
    blocks = lambda n: pltpu.VMEM((n, rows, model), BF)
    landed, rel = pl.pallas_call(
        functools.partial(layer_kernel, dims),
        out_shape=(
            jax.ShapeDtypeStruct((slots, tb, w), BF),
            jax.ShapeDtypeStruct((hand.shape[0], sc, span * nreq, hand.shape[3]), BF),
        ),
        in_specs=[sm, sm, sm, vm, hb, vm, hb, hb, hb, hb, hb, hb, hb, hb, vm, vm, vm, vm],
        out_specs=(vm, hb),
        scratch_shapes=[
            pltpu.VMEM((n8, sc, tokens, w), BF),
            pltpu.VMEM((model, 3 * w), BF),
            pltpu.VMEM((w, model), BF),
            pltpu.VMEM((model, 2 * ff), BF),
            pltpu.VMEM((ff, model), BF),
            pltpu.VMEM(attn_cache.shape, BF),
            pltpu.VMEM((rtot, 3 * w), F32),
            pltpu.VMEM((rtot // 128, 8, 128), F32),
            pltpu.VMEM((n8, rtot // 128, 8, 128), F32),
            pltpu.VMEM((rtot // 128, 8, 128), F32),
            pltpu.VMEM((rtot, w), BF),
            pltpu.VMEM((rtot, w), BF),
            pltpu.VMEM((rtot, w), BF),
            pltpu.VMEM((rtot, w), BF),
            pltpu.VMEM((slots, tb, w), BF),
            pltpu.VMEM(hand.shape, BF),
            pltpu.VMEM(hand.shape, BF),
            pltpu.VMEM((rtot, HD), F32),
            pltpu.VMEM((rtot, HD), F32),
            pltpu.VMEM((nhead, rows, model), F32),
            blocks(nhead), blocks(nhead), blocks(nhead), blocks(nhead),
            blocks(nhead), blocks(nhead), blocks(nhead), blocks(nhead),
            blocks(n8),
            pltpu.VMEM((rows // tb, n8, tb, w), BF),
            dma, dma, dma, dma, dma((9,)), dma, dma((n8,)), dma, dma((n8,)),
            dma, dma((nhead,)), dma, dma((nhead,)), dma, dma((n8,)),
            dma, dma((nhead,)), dma, dma((nhead,)),
            dma, dma,
        ],
        compiler_params=pltpu.CompilerParams(
            collective_id=0, has_side_effects=True, vmem_limit_bytes=56 * 1024 * 1024
        ),
    )(
        slot_request, cache_len, group_len, group_rows, hand, freq, attn_cache, query_weight, key_weight, value_weight,
        out_weight, gate_weight, up_weight, down_weight,
        query_gain[None], key_gain[None], attn_gain[None], mlp_gain[None],
    )
    home = pl.pallas_call(
        home_kernel,
        out_shape=jax.ShapeDtypeStruct((slots, tb, w), BF),
        in_specs=[sm, vm],
        out_specs=vm,
    )(slot_request, landed)
    return (home, rel[None])


def solution(mesh):
    in_specs = (
        P(None, "req", ("head", "blk")),
        P(),
        P(),
        P(),
        P(None, "req", None, ("head", "blk")),
        P("blk", None, None, "req", "head"),
        P(None, ("head", "blk")),
        P(None, ("head", "blk")),
        P(None, ("head", "blk")),
        P(("head", "blk"), None),
        P(("head", "blk")),
        P(("head", "blk")),
        P(),
        P(),
        P(None, ("head", "blk")),
        P(None, ("head", "blk")),
        P(("head", "blk"), None),
    )
    out_specs = (P(None, "req", ("head", "blk")), P("blk", None, "req", None, "head"))
    return jax.shard_map(
        on_device, mesh=mesh, in_specs=in_specs, out_specs=out_specs, check_vma=False
    )
```

```python
import functools

import jax
import jax.numpy as jnp
from jax import lax
from jax.experimental import pallas as pl
from jax.experimental.pallas import tpu as pltpu
from jax.sharding import PartitionSpec as P

HD = 128


EPSILON = 1e-06
ROPE_BASE = 500000.0


BF = jnp.bfloat16
F32 = jnp.float32


def layer_kernel(
    dims,
    slot_ref, clen_ref, glen_ref, group, hand, freq, ac_hbm, wq, wk, wv, wo_hbm, wg, wu, wd_hbm,
    qg, kg, ag, mg,
    landed, rel,
    xfull, wqkv, wo, wgu, wd, ac, qkv, stat_mine, stat_all, scale, qb, kb, vb, attended,
    xt, ht_in, ht, cos_ref, sin_ref, acc, sb1, rb1, sc1, rc1, sb2, rb2, sc2, rc2, stfull, res,
    bsend, xz_recv, h_send, h_recv, lsem, xa_send, xa_recv, st_send, st_recv,
    r1_send, r1_recv, r2_send, r2_recv, sa_send, sa_recv, d1_send, d1_recv, d2_send, d2_recv,
    f_send, f_recv,
):
    nreq, nhead, slots, sc, tokens, tb, w, rows = dims
    model = w * nhead * 2
    rtot = sc * tokens
    r = lax.axis_index("req")
    h = lax.axis_index("head")
    b = lax.axis_index("blk")
    k = h * 2 + b
    other = 1 - b
    span = ht.shape[2]

    def dev(rr, hh, bb):
        return {"req": rr, "head": hh, "blk": bb}

    def rcopy(src, dst, ssem, rsem, rr, hh, bb):
        return pltpu.make_async_remote_copy(
            src_ref=src, dst_ref=dst, send_sem=ssem, recv_sem=rsem,
            device_id=dev(rr, hh, bb), device_id_type=pl.DeviceIdType.MESH,
        )

    barrier = pltpu.get_barrier_semaphore()

    def greet(rr, hh, bb):
        pl.semaphore_signal(
            barrier, inc=1, device_id=dev(rr, hh, bb), device_id_type=pl.DeviceIdType.MESH
        )

    def greet_z(i, carry):
        greet(lax.rem(r + i, nreq), h, b)
        return carry

    lax.fori_loop(1, nreq, greet_z, 0)
    for i in range(1, nhead * 2):
        kk = lax.rem(k + i, nhead * 2)
        greet(r, kk // 2, lax.rem(kk, 2))

    def greet_final(i, carry):
        m = i // nreq
        kk = m * (tokens // rows) + (r * tb) // rows
        rr = lax.rem(i, nreq)

        greet(rr, kk // 2, lax.rem(kk, 2))
        return carry

    lax.fori_loop(0, slots, greet_final, 0)
    first_row = k * rows
    my_slot = first_row // tokens
    my_off = lax.rem(first_row, tokens)
    base_req = my_off // tb
    n_dest = rows // tb
    own_dest = jnp.logical_and(base_req <= r, r < base_req + n_dest)
    locals_ = []

    def load(src, dst, i):
        c = pltpu.make_async_copy(src, dst, lsem.at[i])
        c.start()
        locals_.append(c)

    load(wq, wqkv.at[:, 0:w], 0)
    load(wk, wqkv.at[:, w : 2 * w], 1)
    load(wv, wqkv.at[:, 2 * w : 3 * w], 2)
    load(ac_hbm, ac, 3)
    load(wo_hbm, wo, 4)
    load(wg, wgu.at[:, 0 : wg.shape[1]], 5)
    load(wu, wgu.at[:, wg.shape[1] : 2 * wg.shape[1]], 6)
    load(wd_hbm, wd, 7)
    load(hand, ht_in, 8)

    def order_x(i, carry):
        xt[i] = group[slot_ref[i]]
        return carry

    lax.fori_loop(0, slots, order_x, 0)
    total = (nreq - 1) + (2 * nhead - 1) + slots
    pl.semaphore_wait(barrier, total)

    my_tok = pl.multiple_of(r * tb, tb)

    def send_x(i, carry):
        rr = lax.rem(r + i, nreq)
        rcopy(
            xt.at[pl.ds(rr * sc, sc)], xfull.at[k, :, pl.ds(my_tok, tb)],
            bsend, xz_recv, rr, h, b,
        ).start()
        return carry

    lax.fori_loop(1, nreq, send_x, 0)
    pltpu.make_async_copy(
        xt.at[pl.ds(r * sc, sc)], xfull.at[k, :, pl.ds(my_tok, tb)], xz_recv
    ).start()
    pltpu.make_async_copy(xfull.at[k], xfull.at[k], xz_recv).wait()

    def gather_send(full, ssem, rsem):
        for d in range(1, nhead):
            rcopy(full.at[k], full.at[k], ssem, rsem.at[k], r, lax.rem(h + d, nhead), b).start()
        rcopy(full.at[k], full.at[k], ssem, rsem.at[k], r, h, other).start()

    def got(full, rsem, kk):
        pltpu.make_async_copy(full.at[kk], full.at[kk], rsem.at[kk]).wait()

    def forward(full, ssem, rsem, d):
        kk = lax.rem(h + nhead - d, nhead) * 2 + b
        got(full, rsem, kk)
        rcopy(full.at[kk], full.at[kk], ssem, rsem.at[kk], r, h, other).start()

    gather_send(xfull, xa_send, xa_recv)

    my_pos = pl.multiple_of(r * span, span)
    locals_[8].wait()
    step = min(span, 32)

    def order_h(i, carry):
        s = i // (span // step)
        at = pl.multiple_of(lax.rem(i, span // step) * step, step)
        for c in range(hand.shape[0]):
            ht[c, s, pl.ds(at, step), :] = ht_in[c, slot_ref[s], pl.ds(at, step), :]
        return carry

    lax.fori_loop(0, slots * (span // step), order_h, 0)

    def send_h(i, carry):
        rr = lax.rem(r + i, nreq)
        rcopy(
            ht.at[:, pl.ds(rr * sc, sc)], rel.at[:, :, pl.ds(my_pos, span)],
            h_send, h_recv, rr, h, b,
        ).start()
        return carry

    lax.fori_loop(1, nreq, send_h, 0)
    pltpu.make_async_copy(
        ht.at[:, pl.ds(r * sc, sc)], rel.at[:, :, pl.ds(my_pos, span)], h_recv
    ).start()

    half = HD // 2

    def angles(i, carry):
        here = pl.multiple_of(i * 128, 128)
        s = i // (tokens // 128)
        start = clen_ref[slot_ref[r * sc + s]] + lax.rem(i, tokens // 128) * 128
        place = lax.broadcasted_iota(jnp.int32, (128, HD), 0) + start
        lane = lax.broadcasted_iota(jnp.int32, (128, HD), 1)
        angle = place.astype(F32) * freq[...]
        cos_ref[pl.ds(here, 128), :] = jnp.cos(angle)
        sine = jnp.sin(angle)
        sin_ref[pl.ds(here, 128), :] = jnp.where(lane < half, -sine, sine)
        return carry

    lax.fori_loop(0, rtot // 128, angles, 0)

    tile = 128
    per_slot = tokens // tile

    for d in range(1, nhead):
        forward(xfull, xa_send, xa_recv, d)
    for d in range(nhead):
        got(xfull, xa_recv, lax.rem(h + nhead - d, nhead) * 2 + other)
    for c in locals_[:3]:
        c.wait()

    def project(i, carry):
        s = i // per_slot
        at = pl.multiple_of(lax.rem(i, per_slot) * tile, tile)
        here = pl.multiple_of(i * tile, tile)
        x = jnp.concatenate(
            [xfull[kk, s, pl.ds(at, tile), :] for kk in range(2 * nhead)], axis=1
        )
        y = jnp.dot(x, wqkv[...], preferred_element_type=F32)
        qkv[pl.ds(here, tile), :] = y
        q, kn = y[:, :w], y[:, w : 2 * w]
        lanes = lax.broadcasted_iota(jnp.int32, (tile, tile), 1)
        sums = jnp.where(
            lanes == 0,
            jnp.sum(q * q, axis=1, keepdims=True),
            jnp.where(lanes == 1, jnp.sum(kn * kn, axis=1, keepdims=True), 0.0),
        )
        stat_mine[i] = sums.T[0:8, :]
        return carry

    lax.fori_loop(0, rtot // tile, project, 0)
    for i in range(1, 2 * nhead):
        kk = lax.rem(k + i, 2 * nhead)
        rcopy(
            stat_mine, stat_all.at[k], st_send, st_recv.at[k], r, kk // 2, lax.rem(kk, 2)
        ).start()
    stat_all[k] = stat_mine[...]
    for i in range(1, 2 * nhead):
        kk = lax.rem(k + i, 2 * nhead)
        pltpu.make_async_copy(stat_all.at[kk], stat_all.at[kk], st_recv.at[kk]).wait()
    scale[...] = lax.rsqrt(jnp.sum(stat_all[...], axis=0) / model + EPSILON)

    heads_here = w // HD

    def finish(i, carry):
        here = pl.multiple_of(i * tile, tile)
        sq = jnp.concatenate([scale[i], jnp.zeros((tile - 8, tile), F32)], axis=0).T
        cosv = cos_ref[pl.ds(here, tile), :]
        sinv = sin_ref[pl.ds(here, tile), :]
        q = qkv[pl.ds(here, tile), 0:w] * sq[:, 0:1] * qg[...]
        kn = qkv[pl.ds(here, tile), w : 2 * w] * sq[:, 1:2] * kg[...]
        for hh in range(heads_here):
            cut = slice(hh * HD, (hh + 1) * HD)
            qh, kh = q[:, cut], kn[:, cut]
            qb[pl.ds(here, tile), cut] = (qh * cosv + pltpu.roll(qh, HD // 2, 1) * sinv).astype(BF)
            kb[pl.ds(here, tile), cut] = (kh * cosv + pltpu.roll(kh, HD // 2, 1) * sinv).astype(BF)
        vb[pl.ds(here, tile), :] = qkv[pl.ds(here, tile), 2 * w : 3 * w].astype(BF)
        return carry

    lax.fori_loop(0, rtot // tile, finish, 0)
    locals_[3].wait()
    score_scale = 1.0 / HD**0.5
    ctx = ac.shape[2]
    nt = (((1,), (1,)), ((), ()))

    def attend(i, carry):
        s = i // per_slot
        at = lax.rem(i, per_slot) * tile
        here = pl.multiple_of(i * tile, tile)
        there = pl.multiple_of(s * tokens, tokens)
        old_ok = lax.broadcasted_iota(jnp.int32, (tile, ctx), 1) < clen_ref[slot_ref[r * sc + s]]
        col = lax.broadcasted_iota(jnp.int32, (tile, tokens), 1)
        row = lax.broadcasted_iota(jnp.int32, (tile, tokens), 0) + at
        new_ok = jnp.logical_and(col <= row, col < glen_ref[slot_ref[r * sc + s]])
        for hh in range(heads_here):
            cut = slice(hh * HD, (hh + 1) * HD)
            q = qb[pl.ds(here, tile), cut]
            so = lax.dot_general(q, ac[0, s, :, cut], nt, preferred_element_type=F32) * score_scale
            sn = (
                lax.dot_general(q, kb[pl.ds(there, tokens), cut], nt, preferred_element_type=F32)
                * score_scale
            )
            so = jnp.where(old_ok, so, -1e30)
            sn = jnp.where(new_ok, sn, -1e30)
            top = jnp.maximum(
                jnp.max(so, axis=1, keepdims=True), jnp.max(sn, axis=1, keepdims=True)
            )
            po, pn = jnp.exp(so - top), jnp.exp(sn - top)
            inv = 1.0 / (jnp.sum(po, axis=1, keepdims=True) + jnp.sum(pn, axis=1, keepdims=True))
            o = jnp.dot(
                (po * inv).astype(BF), ac[1, s, :, cut], preferred_element_type=F32
            ) + jnp.dot(
                (pn * inv).astype(BF), vb[pl.ds(there, tokens), cut], preferred_element_type=F32
            )
            attended[pl.ds(here, tile), cut] = o.astype(BF)
        return carry

    locals_[4].wait()

    def pair_send(hh, p0, p1, sb, rb, ssem, rsem):
        mine = jnp.where(b == 0, p0, p1)
        theirs = jnp.where(b == 0, p1, p0)
        acc[hh] = mine
        sb[hh] = theirs.astype(BF)
        rcopy(sb.at[hh], rb.at[hh], ssem, rsem.at[hh], r, h, other).start()

    def chip_send(hh, d, rb, sc_, rc_, rsem, ssem2, rsem2):
        pltpu.make_async_copy(rb.at[hh], rb.at[hh], rsem.at[hh]).wait()
        total = acc[hh] + rb[hh].astype(F32)
        if d == 0:
            acc[hh] = total
        else:
            sc_[hh] = total.astype(BF)
            rcopy(sc_.at[hh], rc_.at[h], ssem2, rsem2.at[h], r, hh, b).start()

    def collect(rc_, rsem2):
        value = acc[h]
        for d in range(1, nhead):
            hh = lax.rem(h + nhead - d, nhead)
            pltpu.make_async_copy(rc_.at[hh], rc_.at[hh], rsem2.at[hh]).wait()
            value = value + rc_[hh].astype(F32)
        return value

    order = list(range(1, nhead)) + [0]
    for d in order:
        hh = lax.rem(h + d, nhead)
        at = pl.multiple_of(hh * 2 * rows, 2 * rows)
        for part in range(2 * rows // tile):
            attend(hh * (2 * rows // tile) + part, 0)
        p = jnp.dot(attended[pl.ds(at, 2 * rows), :], wo[...], preferred_element_type=F32)
        pair_send(hh, p[:rows], p[rows:], sb1, rb1, r1_send, r1_recv)
        if d != 1:
            before = d - 1 if d else nhead - 1
            chip_send(lax.rem(h + before, nhead), before, rb1, sc1, rc1, r1_recv, r2_send, r2_recv)
    chip_send(h, 0, rb1, sc1, rc1, r1_recv, r2_send, r2_recv)
    proj = collect(rc1, r2_recv)
    x_rows = jnp.concatenate(
        [xfull[kk, my_slot, pl.ds(pl.multiple_of(my_off, rows), rows), :] for kk in range(2 * nhead)],
        axis=1,
    ).astype(F32)
    norm = lax.rsqrt(jnp.mean(proj * proj, axis=1, keepdims=True) + EPSILON)
    stfull[k] = (x_rows + proj * norm * ag[...]).astype(BF)
    gather_send(stfull, sa_send, sa_recv)
    for c in locals_[5:8]:
        c.wait()
    ff = wd.shape[0]

    def mlp(hh):
        s = jnp.concatenate([stfull[2 * hh], stfull[2 * hh + 1]], axis=0)
        gu = jnp.dot(s, wgu[...], preferred_element_type=F32)
        g, u = gu[:, :ff], gu[:, ff:]
        inner = (g * jax.nn.sigmoid(g) * u).astype(BF)
        p = jnp.dot(inner, wd[...], preferred_element_type=F32)
        pair_send(hh, p[:rows], p[rows:], sb2, rb2, d1_send, d1_recv)

    got(stfull, sa_recv, h * 2 + other)
    mlp(h)
    for d in range(1, nhead):
        forward(stfull, sa_send, sa_recv, d)
    for d in range(1, nhead):
        hh = lax.rem(h + nhead - d, nhead)
        got(stfull, sa_recv, hh * 2 + other)
        mlp(hh)
        chip_send(hh, d, rb2, sc2, rc2, d1_recv, d2_send, d2_recv)
    chip_send(h, 0, rb2, sc2, rc2, d1_recv, d2_send, d2_recv)
    down = collect(rc2, d2_recv)
    norm = lax.rsqrt(jnp.mean(down * down, axis=1, keepdims=True) + EPSILON)
    result = (stfull[k].astype(F32) + down * norm * mg[...]).astype(BF)
    for kk in range(2 * nhead):
        for i in range(n_dest):
            res[i, kk] = result[i * tb : (i + 1) * tb, kk * w : (kk + 1) * w]
    slot = r * sc + my_slot

    def send_home(i, carry):
        kk = lax.rem(k + i // n_dest, 2 * nhead)
        part = lax.rem(i, n_dest)
        rr = base_req + part
        mine = jnp.logical_and(rr == r, kk == k)

        @pl.when(mine)
        def _():
            c = pltpu.make_async_copy(res.at[part, kk], landed.at[slot], f_recv)
            c.start()

        @pl.when(jnp.logical_not(mine))
        def _():
            rcopy(
                res.at[part, kk], landed.at[slot], f_send, f_recv, rr, kk // 2, lax.rem(kk, 2)
            ).start()

        return carry

    lax.fori_loop(0, 2 * nhead * n_dest, send_home, 0)

    pltpu.make_async_copy(landed, landed, f_recv).wait()
    pltpu.make_async_copy(rel, rel, h_recv).wait()

    def drain(ref, sem):
        pltpu.make_async_copy(ref, ref, sem).wait()

    if nreq > 1:
        drain(xt.at[pl.ds(0, (nreq - 1) * sc)], bsend)
        drain(ht.at[:, pl.ds(0, (nreq - 1) * sc)], h_send)
    drain(xfull.at[pl.ds(0, 2 * nhead - 1)], xa_send)
    drain(stfull.at[pl.ds(0, 2 * nhead - 1)], sa_send)
    drain(stat_all.at[pl.ds(0, 2 * nhead - 1)], st_send)
    drain(sb1, r1_send)
    drain(sb2, d1_send)
    drain(sc1.at[pl.ds(0, nhead - 1)], r2_send)
    drain(sc2.at[pl.ds(0, nhead - 1)], d2_send)

    sent = res.shape[0] * res.shape[1]

    @pl.when(own_dest)
    def _():
        drain(landed.at[pl.ds(0, sent - 1)], f_send)

    @pl.when(jnp.logical_not(own_dest))
    def _():
        drain(landed.at[pl.ds(0, sent)], f_send)


def home_kernel(slot_ref, landed, rel_in, home, rel_out):
    rel_out[...] = rel_in[...]

    def one(s, carry):
        home[slot_ref[s]] = landed[s]
        return carry

    @pl.when(jnp.logical_and(pl.program_id(0) == 0, pl.program_id(1) == 0))
    def _():
        lax.fori_loop(0, landed.shape[0], one, 0)


def on_device(
    group_rows,
    slot_request,
    cache_len,
    group_len,
    attn_cache,
    hand_cache,
    query_weight,
    key_weight,
    value_weight,
    out_weight,
    query_gain,
    key_gain,
    attn_gain,
    mlp_gain,
    gate_weight,
    up_weight,
    down_weight,
):
    nreq = lax.axis_size("req")
    nhead = lax.axis_size("head")
    slots, tb, w = group_rows.shape
    sc = slots // nreq
    tokens = tb * nreq
    rows = sc * tokens // (2 * nhead)
    half = HD // 2
    frequency = ROPE_BASE ** (-(jnp.arange(half, dtype=F32) * 2.0 / HD))
    freq = jnp.concatenate([frequency, frequency])[None]
    hand = hand_cache[0]
    model = w * nhead * 2
    ff = gate_weight.shape[1]
    span = hand.shape[2]
    rtot = sc * tokens
    n8 = 2 * nhead
    dims = (nreq, nhead, slots, sc, tokens, tb, w, rows)
    dma = pltpu.SemaphoreType.DMA
    vm = pl.BlockSpec(memory_space=pltpu.VMEM)
    hb = pl.BlockSpec(memory_space=pl.ANY)
    sm = pl.BlockSpec(memory_space=pltpu.SMEM)
    blocks = lambda n: pltpu.VMEM((n, rows, model), BF)
    landed, rel = pl.pallas_call(
        functools.partial(layer_kernel, dims),
        out_shape=(
            jax.ShapeDtypeStruct((slots, tb, w), BF),
            jax.ShapeDtypeStruct((hand.shape[0], sc, span * nreq, hand.shape[3]), BF),
        ),
        in_specs=[sm, sm, sm, vm, hb, vm, hb, hb, hb, hb, hb, hb, hb, hb, vm, vm, vm, vm],
        out_specs=(vm, hb),
        scratch_shapes=[
            pltpu.VMEM((n8, sc, tokens, w), BF),
            pltpu.VMEM((model, 3 * w), BF),
            pltpu.VMEM((w, model), BF),
            pltpu.VMEM((model, 2 * ff), BF),
            pltpu.VMEM((ff, model), BF),
            pltpu.VMEM(attn_cache.shape, BF),
            pltpu.VMEM((rtot, 3 * w), F32),
            pltpu.VMEM((rtot // 128, 8, 128), F32),
            pltpu.VMEM((n8, rtot // 128, 8, 128), F32),
            pltpu.VMEM((rtot // 128, 8, 128), F32),
            pltpu.VMEM((rtot, w), BF),
            pltpu.VMEM((rtot, w), BF),
            pltpu.VMEM((rtot, w), BF),
            pltpu.VMEM((rtot, w), BF),
            pltpu.VMEM((slots, tb, w), BF),
            pltpu.VMEM(hand.shape, BF),
            pltpu.VMEM(hand.shape, BF),
            pltpu.VMEM((rtot, HD), F32),
            pltpu.VMEM((rtot, HD), F32),
            pltpu.VMEM((nhead, rows, model), F32),
            blocks(nhead), blocks(nhead), blocks(nhead), blocks(nhead),
            blocks(nhead), blocks(nhead), blocks(nhead), blocks(nhead),
            blocks(n8),
            pltpu.VMEM((rows // tb, n8, tb, w), BF),
            dma, dma, dma, dma, dma((9,)), dma, dma((n8,)), dma, dma((n8,)),
            dma, dma((nhead,)), dma, dma((nhead,)), dma, dma((n8,)),
            dma, dma((nhead,)), dma, dma((nhead,)),
            dma, dma,
        ],
        compiler_params=pltpu.CompilerParams(
            collective_id=0, has_side_effects=True, vmem_limit_bytes=56 * 1024 * 1024
        ),
    )(
        slot_request, cache_len, group_len, group_rows, hand, freq, attn_cache, query_weight, key_weight, value_weight,
        out_weight, gate_weight, up_weight, down_weight,
        query_gain[None], key_gain[None], attn_gain[None], mlp_gain[None],
    )
    part = pl.BlockSpec((1, 1) + rel.shape[2:], lambda i, j: (i, j, 0, 0))
    home, rel = pl.pallas_call(
        home_kernel,
        grid=rel.shape[:2],
        out_shape=(
            jax.ShapeDtypeStruct((slots, tb, w), BF),
            jax.ShapeDtypeStruct(rel.shape, BF),
        ),
        in_specs=[sm, pl.BlockSpec((slots, tb, w), lambda i, j: (0, 0, 0)), part],
        out_specs=(pl.BlockSpec((slots, tb, w), lambda i, j: (0, 0, 0)), part),
    )(slot_request, landed, rel)
    return (home, rel[None])


def solution(mesh):
    in_specs = (
        P(None, "req", ("head", "blk")),
        P(),
        P(),
        P(),
        P(None, "req", None, ("head", "blk")),
        P("blk", None, None, "req", "head"),
        P(None, ("head", "blk")),
        P(None, ("head", "blk")),
        P(None, ("head", "blk")),
        P(("head", "blk"), None),
        P(("head", "blk")),
        P(("head", "blk")),
        P(),
        P(),
        P(None, ("head", "blk")),
        P(None, ("head", "blk")),
        P(("head", "blk"), None),
    )
    out_specs = (P(None, "req", ("head", "blk")), P("blk", None, "req", None, "head"))
    return jax.shard_map(
        on_device, mesh=mesh, in_specs=in_specs, out_specs=out_specs, check_vma=False
    )
```
